32 devices in a mesh: block: 4 (over y, core), row: 8 (over z, x).
Axes of the slice: x: 2, y: 2, z: 4, core: 2. Of those that a mesh axis runs over, the one named last changes fastest.
Arguments:
- snapshots: bfloat16 [16384, 1024], P('block', 'row'), may hold values from -6 to 6
- usable_frame_tallies: int32 [64], replicated, may hold values from 64 to 256, as said below
- retained_frequency_slots: int32 [64], replicated, may hold values from 0 to 127, as said below
- modes: bfloat16 [64, 2, 1024, 512], P('block', None, 'row'), may hold values from -0.125 to 0.125
Outputs:
- coefficients: float32 [64, 2, 64, 512], P('row', None, 'block')
- energy: float32 [64, 512], P('block')
The draws below stay inside these ranges and needn't reach their ends.
Inputs may be any that keep to these rules, and one draw needn't show every extreme that they name: Only the first usable_frame_tallies[b] snapshots of block b are valid; some block is full. `retained_frequency_slots`: 64 distinct bins in increasing order; bin 0 and bin 256 // 2 - 1 are always kept.
All inputs are finite; a program needn't handle non-finite values.
Results may differ from the reference program's by a relative error of at most 0.004.
Values may be sent and summed in bfloat16 or wider, within the bound.
A program may use at most 64 MiB of HBM per device.

```python
import jax
import jax.numpy as jnp
from jax import lax

FRAMES_PER_SEG = 256
K = 64
M = 512
BLOCKS = 64
SNAPS = 16384
X = 1024


def draw_usable_frame_tallies(key, part):
    first_key, second_key = jax.random.split(key)
    values = jax.random.randint(first_key, (BLOCKS,), FRAMES_PER_SEG // 4, FRAMES_PER_SEG + 1, dtype=jnp.int32)
    complete_block = jax.random.randint(second_key, (), 0, BLOCKS, dtype=jnp.int32)
    places = jnp.arange(BLOCKS, dtype=jnp.int32)
    return jnp.where(places == complete_block, FRAMES_PER_SEG, values).astype(jnp.int32)


def draw_retained_frequency_slots(key, part):
    shuffled = jax.random.permutation(key, FRAMES_PER_SEG // 2 - 2) + 1
    chosen = shuffled[:K - 2].astype(jnp.int32)
    edges = jnp.array([0, FRAMES_PER_SEG // 2 - 1], dtype=jnp.int32)
    return jnp.sort(jnp.concatenate([edges, chosen])).astype(jnp.int32)


def spiked(values, stream_key, source, target, parts, factor):
    def block_of(axis_at):
        return (jnp.arange(values.shape[axis_at]) // (values.shape[axis_at] // parts)).reshape((-1,) + (1,) * (values.ndim - 1 - axis_at))

    first = jax.random.permutation(stream_key, parts)[block_of(target)]
    second = (block_of(target) + parts // 2) % parts
    return jnp.where((block_of(source) == first) | (block_of(source) == second), factor * values, values)


def shard_levels(key, dims, cuts, least, largest):
    def one(axis_at, parts):
        draws = jax.random.uniform(jax.random.fold_in(jax.random.fold_in(key, 6), axis_at), (parts,), jnp.float32, least / len(cuts), largest / len(cuts))
        return jnp.repeat(jnp.exp(draws), dims[axis_at] // parts).reshape((-1,) + (1,) * (len(dims) - axis_at - 1))

    gain = one(*cuts[0])
    for cut in cuts[1:]:
        gain = gain * one(*cut)
    return gain


def gaussian(own_key, extent, scale, bound, pieces=(), kind=jnp.bfloat16):
    gain = shard_levels(own_key, extent, pieces, -0.22, 0.18) if pieces else 1.0
    entries = jax.random.normal(own_key, extent, jnp.float32) * scale * gain
    return jnp.minimum(jnp.maximum(entries, -bound), bound).astype(kind)


def noise_with(own_key, dims, deviation, reach, cuts, heavy, held_as=jnp.bfloat16):
    values = deviation * jax.random.normal(own_key, dims, jnp.float32)
    if cuts:
        values = values * shard_levels(own_key, dims, cuts, -0.22, 0.18)
    return jnp.clip(spiked(values, jax.random.fold_in(own_key, 3), *heavy), -reach, reach).astype(held_as)


def setup_inputs(seed: int = 0) -> dict:
    keys = jax.random.split(jax.random.key(seed), 5)
    return {
        "snapshots": noise_with(keys[0], (SNAPS, X), 1.0, 6.0, ((0, 4), (1, 8)), (1, 0, 8, 2.0)),
        "usable_frame_tallies": draw_usable_frame_tallies(jax.random.fold_in(keys[4], 71), 0),
        "retained_frequency_slots": draw_retained_frequency_slots(jax.random.fold_in(keys[4], 71), 0),
        "modes": gaussian(keys[3], (K, 2, X, M), (2 * X) ** -0.5, 0.125, ((0, 4), (2, 8))),
    }


def window_table(usable_frame_tallies, retained_frequency_slots):
    recording_epochs = jnp.arange(FRAMES_PER_SEG, dtype=jnp.int32)
    lengths = usable_frame_tallies.astype(jnp.float32)[:, None]
    frequency_power_statistics = recording_epochs.astype(jnp.float32)[None, :]
    domain_grid_locations = recording_epochs[None, :] < usable_frame_tallies[:, None]
    window = jnp.where(domain_grid_locations, jnp.sin(jnp.pi * (frequency_power_statistics + 0.5) / lengths) ** 2, 0.0)
    scaling = 1.0 / jnp.sqrt(lax.optimization_barrier(jnp.sum(window * window, axis=1, keepdims=True)))
    remaining_matrix_lines = retained_frequency_slots[:, None] * recording_epochs[None, :] % FRAMES_PER_SEG
    phase = remaining_matrix_lines.astype(jnp.float32) * (2.0 * jnp.pi / FRAMES_PER_SEG)
    trig = jnp.stack([jnp.cos(phase), -jnp.sin(phase)])
    return ((scaling * window)[:, None, None, :] * trig[None]).astype(jnp.bfloat16)

def reference(snapshots, usable_frame_tallies, retained_frequency_slots, modes):
    table = window_table(usable_frame_tallies, retained_frequency_slots)
    blocks_data = snapshots.reshape(BLOCKS, FRAMES_PER_SEG, X)

    def transform(pair):
        weights, samples = pair
        inner_product = jnp.dot(weights.reshape(2 * K, FRAMES_PER_SEG), samples, preferred_element_type=jnp.float32)
        return inner_product.astype(jnp.bfloat16).reshape(2, K, X)
    spectra = lax.map(transform, (table, blocks_data))
    by_freq = jnp.moveaxis(spectra, 2, 0)

    def project(pair):
        spectrum, mode_rows = pair
        real_part = spectrum[:, 0]
        imag_part = spectrum[:, 1]
        stacked = jnp.concatenate([jnp.concatenate([real_part, imag_part], axis=-1), jnp.concatenate([imag_part, -real_part], axis=-1)], axis=0)
        result = jnp.dot(stacked, mode_rows.reshape(2 * X, M), preferred_element_type=jnp.float32)
        return result.reshape(2, BLOCKS, M)
    projected = lax.map(project, (by_freq, modes))
    coefficients = jnp.transpose(projected, (2, 1, 0, 3))
    weights = usable_frame_tallies.astype(jnp.float32)
    power = coefficients[:, 0] ** 2 + coefficients[:, 1] ** 2
    energy = lax.optimization_barrier(jnp.sum(weights[:, None, None] * power, axis=0)) / jnp.sum(weights)
    return (coefficients, energy)
```

```python
import functools

import jax
import jax.numpy as jnp
from jax import lax
from jax.experimental import pallas as pl
from jax.experimental.pallas import tpu as pltpu
from jax.sharding import PartitionSpec as P

FRAMES_PER_SEG = 256
MESH = pl.DeviceIdType.MESH
F32 = jnp.float32
BF16 = jnp.bfloat16
SWAPPED = (1, 3, 5)
AHEAD = 3
SENT_AHEAD = 10
LANES = 128


def sin_poly(x):
    y = x * x
    s = 1.0 / 6227020800.0
    for c in (-1.0 / 39916800.0, 1.0 / 362880.0, -1.0 / 5040.0, 1.0 / 120.0, -1.0 / 6.0, 1.0):
        s = s * y + c
    return x * s


def cos_poly(x):
    y = x * x
    s = 1.0 / 479001600.0
    for c in (-1.0 / 3628800.0, 1.0 / 40320.0, -1.0 / 720.0, 1.0 / 24.0, -0.5, 1.0):
        s = s * y + c
    return s


def kernel(
    dims,
    tally_ref,
    slot_ref,
    snap_hbm,
    modes_hbm,
    out_ref,
    energy_ref,
    snap,
    modes,
    prod,
    trig,
    wide,
    spec,
    arrived,
    full,
    efull,
    load_sem,
    a_send,
    a_recv,
    r_send,
    r_recv,
    e_send,
    e_recv,
    *stages,
):
    nb, nr, spans, groups, orders = dims
    chunks = len(spans)
    bits = nr.bit_length() - 1
    sends, recvs, eparts = stages[:bits], stages[bits : 2 * bits], stages[2 * bits :]
    frames = FRAMES_PER_SEG
    slots = slot_ref.shape[0]
    blocks = tally_ref.shape[0]
    own_blocks = blocks // nb
    kl = slots // nb
    share = blocks // nr
    m = modes_hbm.shape[3]
    me_b = lax.axis_index("block")
    me_r = lax.axis_index("row")
    mine = [(me_r // (1 << t)) % 2 for t in range(bits)]

    def peer_b(j):
        return lax.rem(me_b + j, nb)

    barrier = pltpu.get_barrier_semaphore()
    for j in range(1, nb):
        pl.semaphore_signal(barrier, inc=1, device_id=(peer_b(j), me_r), device_id_type=MESH)
    partners = [me_r + (1 - 2 * mine[t]) * (1 << t) for t in range(bits)]
    for t in range(bits):
        pl.semaphore_signal(barrier, inc=1, device_id=(me_b, partners[t]), device_id_type=MESH)
    snap_load = pltpu.make_async_copy(snap_hbm, snap, load_sem.at[0])
    snap_load.start()
    modes_load = pltpu.make_async_copy(modes_hbm, modes, load_sem.at[1])
    modes_load.start()

    times = lax.broadcasted_iota(jnp.int32, (1, frames), 1)
    for k in range(slots):
        prod[k : k + 1, :] = (slot_ref[k] * times) & (frames - 1)
    eighth = frames // 8
    turned = prod[...] + eighth
    quarter = (turned >> (eighth.bit_length())) & 3
    angle = ((turned & (2 * eighth - 1)) - eighth).astype(F32) * (2.0 * jnp.pi / frames)
    sn = sin_poly(angle)
    cs = cos_poly(angle)
    odd = (quarter & 1) == 1
    cos_mag = jnp.where(odd, sn, cs)
    sin_mag = jnp.where(odd, cs, sn)
    cos_neg = (quarter == 1) | (quarter == 2)
    trig[0:slots, :] = jnp.where(cos_neg, -cos_mag, cos_mag)
    trig[slots : 2 * slots, :] = jnp.where(quarter >= 2, sin_mag, -sin_mag)

    rows = lax.broadcasted_iota(jnp.int32, (own_blocks, frames), 0)
    cols = lax.broadcasted_iota(jnp.int32, (own_blocks, frames), 1)
    counts = jnp.zeros((own_blocks, frames), jnp.int32)
    for b in range(own_blocks):
        counts = jnp.where(rows == b, tally_ref[me_b * own_blocks + b], counts)
    at = (cols.astype(F32) + 0.5) / counts.astype(F32)
    wave = sin_poly(jnp.pi * jnp.minimum(at, 1.0 - at))
    window = jnp.where(cols < counts, wave * wave, 0.0)
    scaling = 1.0 / jnp.sqrt(jnp.sum(window * window, axis=1, keepdims=True))
    scaled = scaling * window

    snap_load.wait()
    for b in range(own_blocks):
        table = (scaled[b : b + 1, :] * trig[...]).astype(BF16)
        wide[pl.ds(b, 2 * slots, stride=own_blocks), :] = jnp.dot(
            table, snap[b * frames : (b + 1) * frames, :], preferred_element_type=F32
        )

    pl.semaphore_wait(barrier, nb - 1 + bits)

    def part_of(c):
        return pl.ds(*spans[c])

    def keys_of(c):
        return range(spans[c][0], spans[c][0] + spans[c][1])

    def a_copy(c, j):
        to = peer_b(j)
        return pltpu.make_async_remote_copy(
            src_ref=spec.at[to, part_of(c)],
            dst_ref=arrived.at[me_b, part_of(c)],
            send_sem=a_send.at[c, j - 1],
            recv_sem=a_recv.at[c, j - 1],
            device_id=(to, me_r),
            device_id_type=MESH,
        )

    def send_spectra(c):
        for p in range(nb):
            for k in keys_of(c):
                for part in range(2):
                    first = (part * slots + p * kl + k) * own_blocks
                    spec[p, k, part] = wide[first : first + own_blocks, :].astype(BF16)
        for j in range(1, nb):
            a_copy(c, j).start()
        for k in keys_of(c):
            arrived[me_b, k] = spec[me_b, k]

    for c in range(min(SENT_AHEAD, chunks)):
        send_spectra(c)

    def r_copy(c, t):
        bit = orders[c][t]
        src = sends[0].at[1 - mine[bit]] if t == 0 else sends[t]
        return pltpu.make_async_remote_copy(
            src_ref=src.at[:, part_of(c)],
            dst_ref=recvs[t].at[:, part_of(c)],
            send_sem=r_send.at[c, t],
            recv_sem=r_recv.at[c, t],
            device_id=(me_b, partners[bit]),
            device_id_type=MESH,
        )

    def row_of(c, t, q):
        order = orders[c]
        row = sum(mine[bit] * (1 << bit) for bit in order[: t + 1])
        for i, bit in enumerate(order[t + 1 :]):
            row = row + ((q // (1 << i)) % 2) * (1 << bit)
        return row

    def e_copy(h, j):
        to = lax.rem(me_r + j, nr)
        return pltpu.make_async_remote_copy(
            src_ref=eparts[h].at[me_r],
            dst_ref=eparts[h].at[me_r],
            send_sem=e_send.at[h, j - 1],
            recv_sem=e_recv.at[h, j - 1],
            device_id=(me_b, to),
            device_id_type=MESH,
        )

    def e_arrival(h, j):
        source = lax.rem(me_r + nr - j, nr)
        return pltpu.make_async_remote_copy(
            src_ref=eparts[h].at[source],
            dst_ref=eparts[h].at[source],
            send_sem=e_send.at[h, j - 1],
            recv_sem=e_recv.at[h, j - 1],
            device_id=(me_b, lax.rem(me_r + j, nr)),
            device_id_type=MESH,
        )

    def a_arrival(c, j):
        source = lax.rem(me_b + nb - j, nb)
        return pltpu.make_async_remote_copy(
            src_ref=spec.at[peer_b(j), part_of(c)],
            dst_ref=arrived.at[source, part_of(c)],
            send_sem=a_send.at[c, j - 1],
            recv_sem=a_recv.at[c, j - 1],
            device_id=(peer_b(j), me_r),
            device_id_type=MESH,
        )

    modes_load.wait()
    for c in range(chunks):
        for j in range(1, nb):
            a_arrival(c, j).wait_recv()
        if c + SENT_AHEAD < chunks:
            send_spectra(c + SENT_AHEAD)
        for k in keys_of(c):
            re = jnp.concatenate([arrived[s, k, 0] for s in range(nb)], axis=0)
            im = jnp.concatenate([arrived[s, k, 1] for s in range(nb)], axis=0)
            left = jnp.concatenate(
                [jnp.concatenate([re, im], axis=1), jnp.concatenate([im, -re], axis=1)], axis=0
            )
            right = jnp.concatenate([modes[k, 0], modes[k, 1]], axis=0)
            result = jnp.dot(left, right, preferred_element_type=F32)
            for r in range(nr):
                piece = jnp.concatenate(
                    [
                        result[r * share : (r + 1) * share],
                        result[blocks + r * share : blocks + (r + 1) * share],
                    ],
                    axis=0,
                )
                order = orders[c]
                q = sum(((r >> bit) & 1) << i for i, bit in enumerate(order[1:]))
                full[r, k] = piece
                sends[0][(r >> order[0]) & 1, q, k] = piece.astype(BF16)
        if c < AHEAD:
            r_copy(c, 0).start()

    total = tally_ref[0]
    for b in range(1, blocks):
        total = total + tally_ref[b]
    total = total.astype(F32)
    share_rows = lax.broadcasted_iota(jnp.int32, (share, 1), 0)
    weights = jnp.zeros((share, 1), F32)
    for b in range(share):
        weights = jnp.where(share_rows == b, tally_ref[me_r * share + b].astype(F32), weights)

    def finish(k, value):
        for part in range(2):
            for lane in range(m // LANES):
                out_ref[lane, pl.ds(part * kl + k, share, stride=2 * kl), :] = value[
                    part * share : (part + 1) * share, lane * LANES : (lane + 1) * LANES
                ]
        real, imag = value[:share], value[share:]
        power = weights * (real * real + imag * imag)
        efull[k : k + 1, :] = jnp.sum(power, axis=0, keepdims=True)
        for h, (first, size) in enumerate(groups):
            if k == first + size - 1:
                eparts[h][me_r] = efull[first : first + size, :].astype(BF16)
                for j in range(1, nr):
                    e_copy(h, j).start()

    def advance(c, t):
        r_copy(c, t).wait_recv()
        if t == 0 and c + AHEAD < chunks:
            r_copy(c + AHEAD, 0).start()
        if t == bits - 1:
            for k in keys_of(c):
                finish(k, full[me_r, k] + recvs[t][0, k].astype(F32))
            return
        bit = orders[c][t + 1]
        for half in range(2):
            which = mine[bit] if half else 1 - mine[bit]
            for q in range(nr >> (t + 2)):
                piece = 2 * q + which
                row = row_of(c, t, piece)
                for k in keys_of(c):
                    value = full[row, k] + recvs[t][piece, k].astype(F32)
                    if half:
                        full[row, k] = value
                    else:
                        sends[t + 1][q, k] = value.astype(BF16)
            if not half:
                r_copy(c, t + 1).start()

    for step in range(chunks + 2 * (bits - 1)):
        for t in range(bits):
            if 0 <= step - 2 * t < chunks:
                advance(step - 2 * t, t)

    for h, (first, size) in enumerate(groups):
        for j in range(1, nr):
            e_arrival(h, j).wait_recv()
        acc = eparts[h][0].astype(F32)
        for r in range(1, nr):
            acc = acc + eparts[h][r].astype(F32)
        energy_ref[first : first + size, :] = acc / total

    for c in range(chunks):
        for j in range(1, nb):
            a_copy(c, j).wait_send()
        for t in range(bits):
            r_copy(c, t).wait_send()
    for h in range(len(groups)):
        for j in range(1, nr):
            e_copy(h, j).wait_send()


def write_out(values_ref, energy_in, out_hbm, energy_out, sem):
    copies = [pltpu.make_async_copy(energy_in, energy_out, sem.at[0])]
    for lane in range(values_ref.shape[0]):
        copies.append(
            pltpu.make_async_copy(
                values_ref.at[lane],
                out_hbm.at[:, lane * LANES : (lane + 1) * LANES],
                sem.at[lane + 1],
            )
        )
    for copy in copies:
        copy.start()
    for copy in copies:
        copy.wait()


def shards(nb, nr, snapshots, usable_frame_tallies, retained_frequency_slots, modes):
    slots = retained_frequency_slots.shape[0]
    blocks = usable_frame_tallies.shape[0]
    width = snapshots.shape[1]
    kl, _, _, m = modes.shape
    own_blocks = blocks // nb
    share = blocks // nr
    bits = nr.bit_length() - 1
    singles = 0
    sizes = [2] * ((kl - singles) // 2)
    sizes += [1] * (kl - sum(sizes))
    spans = tuple((sum(sizes[:c]), sizes[c]) for c in range(len(sizes)))
    chunks = len(spans)
    plain = tuple(range(bits))
    swapped = (1, 0) + plain[2:]
    orders = tuple(swapped if c in SWAPPED else plain for c in range(chunks))
    late = kl // 2
    groups = ((0, kl - late), (kl - late, late))
    dims = (nb, nr, spans, groups, orders)
    pieces = [(nr >> (t + 1), kl, 2 * share, m) for t in range(bits)]
    dma = pltpu.SemaphoreType.DMA
    smem = pl.BlockSpec(memory_space=pltpu.SMEM)
    anywhere = pl.BlockSpec(memory_space=pl.ANY)
    vmem = pl.BlockSpec(memory_space=pltpu.VMEM)
    values, energy = pl.pallas_call(
        functools.partial(kernel, dims),
        out_shape=(
            jax.ShapeDtypeStruct((m // LANES, 2 * share * kl, LANES), F32),
            jax.ShapeDtypeStruct((kl, m), F32),
        ),
        in_specs=[smem, smem, anywhere, anywhere],
        out_specs=(vmem, vmem),
        scratch_shapes=[
            pltpu.VMEM(snapshots.shape, BF16),
            pltpu.VMEM(modes.shape, BF16),
            pltpu.VMEM((slots, FRAMES_PER_SEG), jnp.int32),
            pltpu.VMEM((2 * slots, FRAMES_PER_SEG), F32),
            pltpu.VMEM((2 * slots * own_blocks, width), F32),
            pltpu.VMEM((nb, kl, 2, own_blocks, width), BF16),
            pltpu.VMEM((nb, kl, 2, own_blocks, width), BF16),
            pltpu.VMEM((nr, kl, 2 * share, m), F32),
            pltpu.VMEM((kl, m), F32),
            dma((2,)),
            dma((chunks, nb - 1)),
            dma((chunks, nb - 1)),
            dma((chunks, bits)),
            dma((chunks, bits)),
            dma((len(groups), nr - 1)),
            dma((len(groups), nr - 1)),
            pltpu.VMEM((2,) + pieces[0], BF16),
        ]
        + [pltpu.VMEM(piece, BF16) for piece in pieces[1:]]
        + [pltpu.VMEM(piece, BF16) for piece in pieces]
        + [pltpu.VMEM((nr, size, m), BF16) for _, size in groups],
        compiler_params=pltpu.CompilerParams(
            collective_id=0, has_side_effects=True, vmem_limit_bytes=24 << 20
        ),
        name="welch",
    )(pltpu.with_memory_space_constraint(usable_frame_tallies, pltpu.HBM), pltpu.with_memory_space_constraint(retained_frequency_slots, pltpu.HBM), pltpu.with_memory_space_constraint(snapshots, pltpu.HBM), pltpu.with_memory_space_constraint(modes, pltpu.HBM))
    out, energy = pl.pallas_call(
        write_out,
        out_shape=(
            jax.ShapeDtypeStruct((2 * share * kl, m), F32),
            jax.ShapeDtypeStruct((kl, m), F32),
        ),
        in_specs=[vmem, vmem],
        out_specs=(anywhere, anywhere),
        scratch_shapes=[dma((m // LANES + 1,))],
        compiler_params=pltpu.CompilerParams(vmem_limit_bytes=1 << 20),
        name="write_out",
    )(values, energy)
    return out.reshape(share, 2, kl, m), energy


def solution(mesh):
    placed = (P("block", "row"), P(), P(), P("block", None, "row", None))
    return jax.shard_map(
        functools.partial(shards, mesh.shape["block"], mesh.shape["row"]),
        mesh=mesh,
        in_specs=placed,
        out_specs=(P("row", None, "block", None), P("block", None)),
        check_vma=False,
    )
```
